512 devices in a mesh: wide: 64 (over y, z_lo, core), rep: 8 (over z_hi, x).
Axes of the slice: x: 4, y: 8, z: 8 (z_hi: 2, z_lo: 4; z = z_hi * 4 + z_lo), core: 2. Of those that a mesh axis runs over, the one named last changes fastest.
Arguments:
- features: bfloat16 [65536, 512], P(('wide', 'rep')), may hold values from -6 to 6
- w_query: bfloat16 [512, 512], replicated, may hold values from -0.25 to 0.25
- w_key: bfloat16 [512, 512], replicated, may hold values from -0.25 to 0.25
- w_out: bfloat16 [512, 512], replicated, may hold values from -0.25 to 0.25
- edge_weight: bfloat16 [64, 8, 96, 128, 128], P('wide', 'rep'), may hold values from -0.23925781 to 0.23925781
- tile_slot: int32 [64, 8, 96], P('wide', 'rep'), may hold values from 0 to 511, as said below
- tile_count: int32 [64, 8], P('wide', 'rep'), may hold values from 1 to 96, as said below
Outputs:
- updated: bfloat16 [65536, 512], P(('wide', 'rep'))
The draws below stay inside these ranges and needn't reach their ends.
Inputs may be any that keep to these rules, and one draw needn't show every extreme that they name: For each w and r the first tile_count[w, r] entries of tile_slot[w, r] are distinct and ascending; all 96 entries of a list are distinct. `tile_count`: some device has 96 live tiles.
All inputs are finite; a program needn't handle non-finite values.
Results may differ from the reference program's by a relative error of at most 0.014.
Values may be sent and summed in bfloat16 or wider, within the bound.
A program may use at most 64 MiB of HBM per device.

```python
import jax
import jax.numpy as jnp
from jax import lax

F = 512
TILE = 128
N_NODES = 65536
TPD = 96
N_WIDE = 64
N_REP = 8


def tile_plan(key):
    base = jax.random.fold_in(key, 7)
    total_slots = N_WIDE * N_REP
    devices = N_WIDE * N_REP
    perm_keys = jax.random.split(jax.random.fold_in(base, 1), devices)
    perms = jax.vmap(lambda single: jax.random.permutation(single, total_slots)[:TPD])(perm_keys).astype(jnp.int32)
    levels = jax.random.randint(jax.random.fold_in(base, 2), (devices,), 0, 3).astype(jnp.int32)
    counts = jnp.maximum(TPD // jnp.left_shift(jnp.int32(1), levels), 1).astype(jnp.int32)
    busiest = jax.random.randint(jax.random.fold_in(base, 3), (), 0, devices)
    counts = jnp.where(jnp.arange(devices) == busiest, TPD, counts).astype(jnp.int32)
    order_key = jnp.where(jnp.arange(TPD)[None, :] < counts[:, None], perms, perms + total_slots)
    order = jnp.argsort(order_key, axis=1, stable=True)
    slots = jnp.take_along_axis(perms, order, axis=1)
    return (slots.reshape(N_WIDE, N_REP, TPD).astype(jnp.int32), counts.reshape(N_WIDE, N_REP))


def draw_tile_slot(key, part):
    return tile_plan(key)[0]


def draw_tile_count(key, part):
    return tile_plan(key)[1]


def steps_of(key, dims, cuts, smallest, largest):
    gain, own = 1.0, jax.random.fold_in(key, 6)
    for axis_at, parts in cuts:
        steps = jnp.exp(jax.random.uniform(jax.random.fold_in(own, axis_at), (parts,), jnp.float32, smallest / len(cuts), largest / len(cuts)))
        gain = gain * jnp.repeat(steps, dims[axis_at] // parts).reshape([-1 if axis == axis_at else 1 for axis in range(len(dims))])
    return gain


def normal_values(own_key, dims, scale, bound, shards=(), held_as=jnp.bfloat16):
    loudness = steps_of(own_key, dims, shards, -0.22, 0.18) if shards else 1.0
    drawn = jax.random.normal(own_key, dims, jnp.float32) * scale * loudness
    return jnp.minimum(jnp.maximum(drawn, -bound), bound).astype(held_as)


def setup_inputs(seed: int = 0) -> dict:
    keys = jax.random.split(jax.random.key(seed), 8)
    features = normal_values(keys[0], (N_NODES, F), 1.0, 6.0, ((0, 512),))
    w_query = normal_values(keys[1], (F, F), F ** -0.5, 0.25)
    w_key = normal_values(keys[2], (F, F), F ** -0.5, 0.25)
    w_out = normal_values(keys[3], (F, F), F ** -0.5, 0.25)
    edge_weight = normal_values(keys[4], (N_WIDE, N_REP, TPD, TILE, TILE), 0.04, 0.23925781, ((0, 64), (1, 8)))
    tile_slot = draw_tile_slot(jax.random.fold_in(keys[7], 71), 0)
    tile_count = draw_tile_count(jax.random.fold_in(keys[7], 71), 0)
    return {"features": features, "w_query": w_query, "w_key": w_key, "w_out": w_out, "edge_weight": edge_weight, "tile_slot": tile_slot, "tile_count": tile_count}


def reference(features, w_query, w_key, w_out, edge_weight, tile_slot, tile_count):
    node_count = features.shape[0]
    query_rows = jnp.dot(features, w_query, preferred_element_type=jnp.float32).astype(jnp.bfloat16)
    key_rows = jnp.dot(features, w_key, preferred_element_type=jnp.float32).astype(jnp.bfloat16)
    query_blocks = query_rows.reshape(N_WIDE * N_REP, TILE, F)
    key_blocks = key_rows.reshape(N_WIDE * N_REP, TILE, F)
    factor = 1.0 / math_sqrt(F)

    def per_device(partial_value, device_num):
        wide_pos = device_num // N_REP
        rep_pos = device_num % N_REP
        tile_slots = tile_slot[wide_pos, rep_pos]
        live_count = tile_count[wide_pos, rep_pos]
        weights = edge_weight[wide_pos, rep_pos].astype(jnp.float32)
        step_of = tile_slots // N_REP
        row_block = (wide_pos * N_REP + tile_slots % N_REP).astype(jnp.int32)
        col_block = ((wide_pos - step_of) % N_WIDE * N_REP + rep_pos).astype(jnp.int32)
        receiver = query_blocks[row_block].astype(jnp.float32)
        sender = key_blocks[col_block].astype(jnp.float32)
        scores = jnp.einsum('tif,tjf->tij', receiver, sender) * factor
        weighted = (jnp.tanh(scores) * weights).astype(jnp.bfloat16)
        weighted = lax.optimization_barrier(weighted).astype(jnp.float32)
        contrib = jnp.einsum('tij,tjf->tif', weighted, sender)
        active = (jnp.arange(TPD, dtype=jnp.int32) < live_count).astype(jnp.float32)
        contrib = contrib * active[:, None, None]
        return (partial_value.at[row_block].add(contrib), None)
    partial_value = jnp.zeros((N_WIDE * N_REP, TILE, F), jnp.float32)
    partial_value = lax.scan(per_device, partial_value, jnp.arange(N_WIDE * N_REP, dtype=jnp.int32))[0]
    message = partial_value.reshape(node_count, F).astype(jnp.bfloat16)
    mixed = features.astype(jnp.float32) + jnp.dot(message, w_out, preferred_element_type=jnp.float32)
    return mixed.astype(jnp.bfloat16)

def math_sqrt(value):
    return float(value) ** 0.5
```

```python
import jax
import jax.numpy as jnp
from jax import lax
from jax.experimental import pallas as pl
from jax.experimental.pallas import tpu as pltpu
from jax.sharding import PartitionSpec as P

F32 = jnp.float32
BF16 = jnp.bfloat16


def tiles_kernel(slot_ref, count_ref, query_ref, source_ref, weight_ref, out_ref, total):
    n_rep, _, width = query_ref.shape
    factor = 1.0 / float(width) ** 0.5
    total[...] = jnp.zeros_like(total)

    def one_tile(t, carry):
        slot = slot_ref[t]
        row = lax.rem(slot, n_rep)
        step = lax.div(slot, n_rep)
        source = source_ref[step]
        scores = lax.dot_general(
            query_ref[row], source, (((1,), (1,)), ((), ())), preferred_element_type=F32
        )
        weighted = (jnp.tanh(scores * factor) * weight_ref[t].astype(F32)).astype(BF16)
        total[row] += jnp.dot(weighted, source, preferred_element_type=F32)
        return carry

    lax.fori_loop(0, count_ref[0], one_tile, 0)
    out_ref[...] = total[...].astype(BF16)


def on_device(features, w_query, w_key, w_out, edge_weight, tile_slot, tile_count):
    rows, width = features.shape
    n_wide = lax.axis_size("wide")
    n_rep = lax.axis_size("rep")
    query_rows = jnp.dot(features, w_query, preferred_element_type=F32).astype(BF16)
    key_rows = jnp.dot(features, w_key, preferred_element_type=F32).astype(BF16)
    sources = lax.all_gather(key_rows, "wide", axis=0)
    receivers = lax.all_gather(query_rows, "rep", axis=0)
    slots = tile_slot[0, 0]
    me = lax.axis_index("wide")
    slots = (me - slots // n_rep) % n_wide * n_rep + slots % n_rep
    partial = pl.pallas_call(
        tiles_kernel,
        out_shape=jax.ShapeDtypeStruct((n_rep, rows, width), BF16),
        in_specs=[pl.BlockSpec(memory_space=pltpu.SMEM)] * 2
        + [pl.BlockSpec(memory_space=pltpu.VMEM)] * 3,
        out_specs=pl.BlockSpec(memory_space=pltpu.VMEM),
        scratch_shapes=[pltpu.VMEM((n_rep, rows, width), F32)],
        compiler_params=pltpu.CompilerParams(vmem_limit_bytes=40 * 2**20),
    )(slots, tile_count[0], receivers, sources, edge_weight[0, 0])
    summed = lax.psum_scatter(
        partial.reshape(n_rep * rows, width), "rep", scatter_dimension=0, tiled=True
    )
    mixed = features.astype(F32) + jnp.dot(summed, w_out, preferred_element_type=F32)
    return mixed.astype(BF16)


def solution(mesh):
    in_specs = (
        P(("wide", "rep"), None),
        P(),
        P(),
        P(),
        P("wide", "rep", None, None, None),
        P("wide", "rep", None),
        P("wide", "rep"),
    )
    out_specs = P(("wide", "rep"), None)
    return jax.shard_map(
        on_device, mesh=mesh, in_specs=in_specs, out_specs=out_specs, check_vma=False
    )
```

```python
import functools

import jax
import jax.numpy as jnp
from jax import lax
from jax.experimental import pallas as pl
from jax.experimental.pallas import tpu as pltpu
from jax.sharding import PartitionSpec as P

F32 = jnp.float32
BF16 = jnp.bfloat16
MESH = pl.DeviceIdType.MESH

NY, NZ, NX = 8, 4, 4


def layer_kernel(
    feat, w_query, w_key, w_out, edge, inv, out,
    src, qry, wts, total, pbuf, part, far, near, merged, joined, zbuf,
    recv, send_p, send_s, send_z, send_c, qrecv, qsend, xrecv, xsend, local,
):
    n_wide = src.shape[0]
    rows, width = feat.shape
    n_live = edge.shape[0]
    factor = 1.0 / float(width) ** 0.5
    w, r = lax.axis_index("wide"), lax.axis_index("rep")
    c, zl, y = w % 2, (w // 2) % NZ, w // 8
    zh, x = r // NX, r % NX
    zo = 1 - zh
    sgn = 1 - 2 * c

    def block_of(yy, zz):
        return ((yy + 2 * NY) % NY) * 8 + (zz % NZ) * 2 + c

    def rep_of(zz, xx):
        return zz * NX + (xx + NX) % NX

    ahead = (block_of(y + sgn, zl), r)
    behind = (block_of(y - sgn, zl), r)
    partner = (w + sgn, r)
    z_peers = [(block_of(y, zl + k), r) for k in (1, 2, 3)]
    x_ahead = (w, rep_of(zh, x + sgn))
    x_behind = (w, rep_of(zh, x - sgn))
    z_far = (w, rep_of(zo, x))

    def remote(a, b, s_sem, r_sem, device):
        return pltpu.make_async_remote_copy(
            src_ref=a, dst_ref=b, send_sem=s_sem, recv_sem=r_sem,
            device_id=device, device_id_type=MESH,
        )

    def move(b, s_sem, device):
        return remote(src.at[b], src.at[b], s_sem, recv.at[b], device)

    def qmove(b, k, device):
        return remote(qry.at[b], qry.at[b], qsend.at[k], qrecv.at[b], device)

    barrier = pltpu.get_barrier_semaphore()
    talk = [ahead, behind, partner] + z_peers + [x_ahead, x_behind, z_far]
    for device in talk:
        pl.semaphore_signal(barrier, inc=1, device_id=device, device_id_type=MESH)

    load = pltpu.make_async_copy(edge, wts.at[pl.ds(0, n_live)], local)
    load.start()
    wts[n_live] = jnp.zeros(wts.shape[1:], BF16)
    src[w] = jnp.dot(feat[...], w_key[...], preferred_element_type=F32).astype(BF16)
    qry[r] = jnp.dot(feat[...], w_query[...], preferred_element_type=F32).astype(BF16)
    total[...] = jnp.zeros_like(total)
    pl.semaphore_wait(barrier, len(talk))

    def got(b):
        move(b, send_p.at[0], ahead).wait_recv()

    def qgot(b):
        qmove(b, 0, x_ahead).wait_recv()

    def hold_first(b, k):
        move(b, send_p.at[k], ahead).start()
        move(b, send_s.at[k], behind).start()
        move(b, send_c.at[2 * k], partner).start()

    def event(dd, j):
        if dd == 0:
            b = block_of(y, zl + j)
            got(b)
            hold_first(b, j)
        else:
            b = block_of(y + sgn * dd, zl + j)
            got(b)
            if dd < 3:
                move(b, send_s.at[4 * dd + j], behind).start()
            move(b, send_c.at[2 * (4 * dd + j)], partner).start()
        forward(dd, j)

    def forward(dd, j):
        b = block_of(y - sgn * (dd + 1), zl + j)
        got(b)
        if dd < 3:
            move(b, send_p.at[4 * dd + 4 + j], ahead).start()
        move(b, send_c.at[2 * (4 * dd + j) + 1], partner).start()

    def pair(n):
        m, side = n // 2, n % 2
        dd, j = m // 4, m % 4
        b = block_of(y + sgn * (dd - side * (2 * dd + 1)), zl + j)
        got(b + sgn)
        base = b - c
        both = jnp.concatenate([src[base], src[base + 1]], axis=0)
        for half in range(2):
            scores = lax.dot_general(
                qry[pl.ds(4 * half, 4)].reshape(4 * rows, width), both,
                (((1,), (1,)), ((), ())), preferred_element_type=F32,
            )
            for i in range(4):
                for k in range(2):
                    slot = ((w - base - k + n_wide) % n_wide) * 8 + 4 * half + i
                    tile = wts[inv[slot]].astype(F32)
                    piece = scores[i * rows:(i + 1) * rows, k * rows:(k + 1) * rows]
                    pbuf[half, i * rows:(i + 1) * rows, k * rows:(k + 1) * rows] = (
                        jnp.tanh(piece * factor) * tile
                    ).astype(BF16)
            total[pl.ds(4 * half, 4)] += jnp.dot(
                pbuf[half], both, preferred_element_type=F32
            ).reshape(4, rows, width)

    def loop(lo, hi, body):
        def step(i, carry):
            body(i)
            return carry

        lax.fori_loop(lo, hi, step, 0)

    hold_first(w, 0)
    for k in range(3):
        move(w, send_z.at[k], z_peers[k]).start()
    qmove(r, 0, z_far).start()
    qmove(r, 1, x_ahead).start()
    qmove(r, 2, x_behind).start()
    forward(0, 0)
    loop(1, 4, lambda j: event(0, j))
    qgot(rep_of(zh, x - sgn))
    qmove(rep_of(zh, x - sgn), 3, x_ahead).start()
    loop(0, 2, lambda j: event(1, j))
    qgot(rep_of(zo, x))
    qmove(rep_of(zo, x), 4, x_ahead).start()
    qmove(rep_of(zo, x), 5, x_behind).start()
    loop(2, 4, lambda j: event(1, j))
    qgot(rep_of(zo, x - sgn))
    qmove(rep_of(zo, x - sgn), 6, x_ahead).start()
    event(2, 0)
    for zz in (zh, zo):
        qgot(rep_of(zz, x + sgn))
        qgot(rep_of(zz, x + 2))
    load.wait()

    loop(0, 4, pair)

    def third(j):
        event(2, j)
        loop(0, 4, lambda i: pair(4 * j + i))

    def fourth(j):
        event(3, j)
        loop(0, 2, lambda i: pair(16 + 2 * j + i))
        loop(0, 2, lambda i: pair(24 + 2 * j + i))

    loop(1, 4, third)
    loop(0, 4, fourth)

    def xcopy(a, b, k, device):
        return remote(a, b, xsend.at[k], xrecv.at[k], device)

    zs = (zo, zh)
    part[...] = total[...].astype(BF16)
    c_far = [xcopy(part.at[rep_of(zs[k], x + 2)], far.at[k], k, x_ahead) for k in (0, 1)]
    c_near = [xcopy(part.at[rep_of(zs[k], x - sgn)], near.at[k], 2 + k, x_behind) for k in (0, 1)]
    c_join = [xcopy(merged.at[k], joined.at[k], 4 + k, x_ahead) for k in (0, 1)]
    c_z = xcopy(zbuf.at[0], zbuf.at[1], 6, z_far)
    for k in (0, 1):
        c_far[k].start()
        c_near[k].start()
    for k in (0, 1):
        c_far[k].wait_recv()
        merged[k] = (total[rep_of(zs[k], x + sgn)] + far[k].astype(F32)).astype(BF16)
        c_join[k].start()

    def mine(k):
        c_near[k].wait_recv()
        c_join[k].wait_recv()
        return total[rep_of(zs[k], x)] + near[k].astype(F32) + joined[k].astype(F32)

    zbuf[0] = mine(0).astype(BF16)
    c_z.start()
    own = mine(1)
    c_z.wait_recv()
    message = (own + zbuf[1].astype(F32)).astype(BF16)
    out[...] = (
        feat[...].astype(F32) + jnp.dot(message, w_out[...], preferred_element_type=F32)
    ).astype(BF16)

    for copy in c_far + c_near + c_join + [c_z]:
        copy.wait_send()
    loop(0, 16, lambda k: move(w, send_p.at[k], ahead).wait_send())
    loop(0, 12, lambda k: move(w, send_s.at[k], behind).wait_send())
    loop(0, 3, lambda k: move(w, send_z.at[k], ahead).wait_send())
    loop(0, 32, lambda k: move(w, send_c.at[k], partner).wait_send())
    loop(0, 7, lambda k: qmove(r, k, x_ahead).wait_send())


def on_device(features, w_query, w_key, w_out, edge_weight, tile_slot, tile_count):
    rows, width = features.shape
    n_wide = lax.axis_size("wide")
    n_rep = lax.axis_size("rep")
    weights = edge_weight[0, 0]
    n_live = weights.shape[0]
    order = jnp.arange(n_live, dtype=jnp.int32)
    hit = (tile_slot[0, 0][None, :] == jnp.arange(n_wide * n_rep, dtype=jnp.int32)[:, None]) & (
        order < tile_count[0, 0]
    )[None, :]
    inv = jnp.min(jnp.where(hit, order[None, :], n_live), axis=1)
    vmem = pl.BlockSpec(memory_space=pltpu.VMEM)
    dma = pltpu.SemaphoreType.DMA
    return pl.pallas_call(
        layer_kernel,
        out_shape=jax.ShapeDtypeStruct((rows, width), BF16),
        in_specs=[vmem] * 4
        + [pl.BlockSpec(memory_space=pl.ANY), pl.BlockSpec(memory_space=pltpu.SMEM)],
        out_specs=vmem,
        scratch_shapes=[
            pltpu.VMEM((n_wide, rows, width), BF16),
            pltpu.VMEM((n_rep, rows, width), BF16),
            pltpu.VMEM((n_live + 1, rows, rows), BF16),
            pltpu.VMEM((n_rep, rows, width), F32),
            pltpu.VMEM((2, 4 * rows, 2 * rows), BF16),
            pltpu.VMEM((n_rep, rows, width), BF16),
            pltpu.VMEM((2, rows, width), BF16),
            pltpu.VMEM((2, rows, width), BF16),
            pltpu.VMEM((2, rows, width), BF16),
            pltpu.VMEM((2, rows, width), BF16),
            pltpu.VMEM((2, rows, width), BF16),
            dma((n_wide,)), dma((16,)), dma((12,)), dma((3,)), dma((32,)),
            dma((n_rep,)), dma((7,)), dma((7,)), dma((7,)), dma,
        ],
        compiler_params=pltpu.CompilerParams(
            collective_id=0, has_side_effects=True, vmem_limit_bytes=56 * 2**20
        ),
    )(features, w_query, w_key, w_out, weights, inv)


def solution(mesh):
    in_specs = (
        P(("wide", "rep"), None),
        P(),
        P(),
        P(),
        P("wide", "rep", None, None, None),
        P("wide", "rep", None),
        P("wide", "rep"),
    )
    out_specs = P(("wide", "rep"), None)
    return jax.shard_map(
        on_device, mesh=mesh, in_specs=in_specs, out_specs=out_specs, check_vma=False
    )
```

```python
import jax
import jax.numpy as jnp
from jax import lax
from jax.experimental import pallas as pl
from jax.experimental.pallas import tpu as pltpu
from jax.sharding import PartitionSpec as P

F32 = jnp.float32
BF16 = jnp.bfloat16
MESH = pl.DeviceIdType.MESH

NY, NZ, NX = 8, 4, 4
ROWS_A = 96


def layer_kernel(
    feat, w_query, w_key, w_out, edge, inv, out,
    src, qry, wts, total, pbuf, part, far, near, merged, joined, zbuf,
    recv_a, recv_b, recv_c, ring_pa, ring_sa, ring_pb, ring_sb, line_a, line_b, send_c,
    qrecv, qsend, xrecv, xsend, local,
):
    n_wide = src.shape[0]
    rows, width = feat.shape
    n_live = edge.shape[0]
    factor = 1.0 / float(width) ** 0.5
    w, r = lax.axis_index("wide"), lax.axis_index("rep")
    c, zl, y = w % 2, (w // 2) % NZ, w // 8
    zh, x = r // NX, r % NX
    zo = 1 - zh
    sgn = 1 - 2 * c
    top = zl // 2
    inner = zl * (1 - top) + (NZ - 1 - zl) * top

    def block_of(yy, zz):
        return ((yy + 2 * NY) % NY) * 8 + zz * 2 + c

    def rep_of(zz, xx):
        return zz * NX + (xx + NX) % NX

    def line_at(p):
        return top * (NZ - 1) + (1 - 2 * top) * (p + inner * (1 - p // 2) * (1 - 2 * p))

    ahead = (block_of(y + sgn, zl), r)
    behind = (block_of(y - sgn, zl), r)
    partner = (w + sgn, r)
    above, below = (w + 2, r), (w - 2, r)
    x_ahead = (w, rep_of(zh, x + sgn))
    x_behind = (w, rep_of(zh, x - sgn))
    x_far = (w, rep_of(zh, x + 2))
    z_far = (w, rep_of(zo, x))
    has_above, has_below = zl < NZ - 1, zl > 0

    def remote(a, b, s_sem, r_sem, device):
        return pltpu.make_async_remote_copy(
            src_ref=a, dst_ref=b, send_sem=s_sem, recv_sem=r_sem,
            device_id=device, device_id_type=MESH,
        )

    def move_a(b, s_sem, device):
        ref = src.at[b, pl.ds(0, ROWS_A)]
        return remote(ref, ref, s_sem, recv_a.at[b // 2], device)

    def move_b(b, s_sem, device):
        ref = src.at[b, pl.ds(ROWS_A, rows - ROWS_A)]
        return remote(ref, ref, s_sem, recv_b.at[b // 2], device)

    def move_c(b, s_sem):
        return remote(src.at[b], src.at[b], s_sem, recv_c.at[b // 2], partner)

    def qmove(b, k, device):
        return remote(qry.at[b], qry.at[b], qsend.at[k], qrecv.at[b], device)

    barrier = pltpu.get_barrier_semaphore()

    def greet(device):
        pl.semaphore_signal(barrier, inc=1, device_id=device, device_id_type=MESH)

    talk = [ahead, behind, partner, x_ahead, x_behind, x_far, z_far]
    for device in talk:
        greet(device)

    @pl.when(has_above)
    def _():
        greet(above)

    @pl.when(has_below)
    def _():
        greet(below)

    load = pltpu.make_async_copy(edge, wts.at[pl.ds(0, n_live)], local)
    load.start()
    wts[n_live] = jnp.zeros(wts.shape[1:], BF16)
    src[w] = jnp.dot(feat[...], w_key[...], preferred_element_type=F32).astype(BF16)
    qry[r] = jnp.dot(feat[...], w_query[...], preferred_element_type=F32).astype(BF16)
    total[...] = jnp.zeros_like(total)
    pl.semaphore_wait(barrier, len(talk) + 1 + inner)

    def line_pass(move, b, zz, sems, k):
        @pl.when((zz <= zl) & has_above)
        def _():
            move(b, sems.at[2 * k], above).start()

        @pl.when((zz >= zl) & has_below)
        def _():
            move(b, sems.at[2 * k + 1], below).start()

    def got_a(b):
        move_a(b, ring_pa.at[0], ahead).wait_recv()

    def got_b(b):
        move_b(b, ring_pb.at[0], ahead).wait_recv()

    def qgot(b):
        qmove(b, 0, x_ahead).wait_recv()

    def take_near(m):
        zz = line_at(m)
        b = block_of(y, zz)
        if m:
            got_a(b)
        move_a(b, ring_pa.at[m], ahead).start()
        move_a(b, ring_sa.at[m], behind).start()
        line_pass(move_a, b, zz, line_a, m)
        if m:
            got_b(b)
        else:
            qmove(r, 0, z_far).start()
            move_b(b, ring_pb.at[0], ahead).start()
            move_b(b, ring_sb.at[0], behind).start()
        line_pass(move_b, b, zz, line_b, m)
        move_c(b, send_c.at[m]).start()

    def take_second(m):
        d, p = m // NZ, m % NZ
        zz = line_at(p)
        b = block_of(y + sgn * d, zz)
        got_a(b)

        @pl.when(d < 3)
        def _():
            move_a(b, ring_sa.at[m], behind).start()

        got_b(b)

        @pl.when((p == 0) & (d < 3))
        def _():
            move_b(b, ring_sb.at[d], behind).start()

        line_pass(move_b, b, zz, line_b, m)
        move_c(b, send_c.at[m]).start()

    def take_first(n):
        d, p = 1 + n // NZ, n % NZ
        zz = line_at(p)
        b = block_of(y - sgn * d, zz)
        got_a(b)

        @pl.when(d < 4)
        def _():
            move_a(b, ring_pa.at[NZ + n], ahead).start()

        got_b(b)

        @pl.when((p == 0) & (d < 4))
        def _():
            move_b(b, ring_pb.at[d], ahead).start()

        line_pass(move_b, b, zz, line_b, 16 + n)
        move_c(b, send_c.at[16 + n]).start()

    def event(n):
        take_second(NZ + n)
        take_first(n)

    def near_block(p):
        return block_of(y, line_at(p))

    def second_block(n):
        return block_of(y + sgn * (1 + n // NZ), line_at(n % NZ))

    def first_block(n):
        return block_of(y - sgn * (1 + n // NZ), line_at(n % NZ))

    def tiles(b1, b2, first, count, wait=True):
        if wait:
            for b in (b1, b2):
                move_c(b + sgn, send_c.at[0]).wait_recv()
        blocks = [b1 - c, b1 - c + 1, b2 - c, b2 - c + 1]
        sources = jnp.concatenate([src[b] for b in blocks], axis=0)
        scores = lax.dot_general(
            qry[pl.ds(first, count)].reshape(count * rows, width), sources,
            (((1,), (1,)), ((), ())), preferred_element_type=F32,
        )
        for i in range(count):
            for k in range(4):
                slot = ((w - blocks[k] + n_wide) % n_wide) * 8 + first + i
                tile = wts[inv[slot]].astype(F32)
                piece = scores[i * rows:(i + 1) * rows, k * rows:(k + 1) * rows]
                pbuf[i * rows:(i + 1) * rows, k * rows:(k + 1) * rows] = (
                    jnp.tanh(piece * factor) * tile
                ).astype(BF16)
        total[pl.ds(first, count)] += jnp.dot(
            pbuf[:count * rows], sources, preferred_element_type=F32
        ).reshape(count, rows, width)

    def ring_tiles(n):
        tiles(second_block(n), first_block(n), 0, 8)

    def loop(lo, hi, body):
        def step(i, carry):
            body(i)
            return carry

        lax.fori_loop(lo, hi, step, 0)

    take_near(0)
    qmove(r, 1, x_ahead).start()
    qmove(r, 2, x_behind).start()
    qmove(r, 3, x_far).start()
    take_near(1)
    event(0)
    take_near(2)
    event(1)
    take_near(3)
    event(2)
    qz = rep_of(zo, x)
    qgot(qz)
    qmove(qz, 4, x_ahead).start()
    qmove(qz, 5, x_behind).start()
    qmove(qz, 6, x_far).start()
    loop(3, 6, event)
    for zz in (zh, zo):
        for k in (sgn, -sgn, 2):
            qgot(rep_of(zz, x + k))
    load.wait()
    loop(0, 2, lambda k: tiles(near_block(2 * k), near_block(2 * k + 1), 0, 8))

    def both(n):
        event(n)
        loop(2 * n - 12, 2 * n - 10, ring_tiles)

    loop(6, 12, both)
    take_first(12)
    take_first(13)
    tiles(first_block(12), first_block(13), 0, 8)
    take_first(14)
    take_first(15)

    def xcopy(a, b, k, device):
        return remote(a, b, xsend.at[k], xrecv.at[k], device)

    zs = (zo, zh)
    c_far = [xcopy(part.at[rep_of(zs[k], x + 2)], far.at[k], k, x_ahead) for k in (0, 1)]
    c_near = [xcopy(part.at[rep_of(zs[k], x - sgn)], near.at[k], 2 + k, x_behind) for k in (0, 1)]
    c_join = [xcopy(merged.at[k], joined.at[k], 4 + k, x_ahead) for k in (0, 1)]
    c_z = xcopy(zbuf.at[0], zbuf.at[1], 6, z_far)

    for k in (0, 1):
        tiles(first_block(14), first_block(15), 4 * zs[k], 4, k == 0)
        for place in (rep_of(zs[k], x + 2), rep_of(zs[k], x - sgn)):
            part[place] = total[place].astype(BF16)
        c_far[k].start()
        c_near[k].start()
    for k in (0, 1):
        c_far[k].wait_recv()
        merged[k] = (total[rep_of(zs[k], x + sgn)] + far[k].astype(F32)).astype(BF16)
        c_join[k].start()

    def mine(k):
        c_near[k].wait_recv()
        c_join[k].wait_recv()
        return total[rep_of(zs[k], x)] + near[k].astype(F32) + joined[k].astype(F32)

    zbuf[0] = mine(0).astype(BF16)
    c_z.start()
    own = mine(1)
    c_z.wait_recv()
    message = (own + zbuf[1].astype(F32)).astype(BF16)
    out[...] = (
        feat[...].astype(F32) + jnp.dot(message, w_out[...], preferred_element_type=F32)
    ).astype(BF16)

    for copy in c_far + c_near + c_join + [c_z]:
        copy.wait_send()
    loop(0, 16, lambda k: move_a(w, ring_pa.at[k], ahead).wait_send())
    loop(0, 12, lambda k: move_a(w, ring_sa.at[k], behind).wait_send())
    loop(0, 4, lambda k: move_b(w, ring_pb.at[k], ahead).wait_send())
    loop(0, 3, lambda k: move_b(w, ring_sb.at[k], behind).wait_send())
    loop(0, 32, lambda k: move_c(w, send_c.at[k]).wait_send())
    loop(0, 7, lambda k: qmove(r, k, x_ahead).wait_send())

    def line_sent(move, sems, k):
        zz = line_at(k % NZ)

        @pl.when((zz <= zl) & has_above)
        def _():
            move(w, sems.at[2 * k], above).wait_send()

        @pl.when((zz >= zl) & has_below)
        def _():
            move(w, sems.at[2 * k + 1], below).wait_send()

    loop(0, 4, lambda k: line_sent(move_a, line_a, k))
    loop(0, 32, lambda k: line_sent(move_b, line_b, k))


def on_device(features, w_query, w_key, w_out, edge_weight, tile_slot, tile_count):
    rows, width = features.shape
    n_wide = lax.axis_size("wide")
    n_rep = lax.axis_size("rep")
    weights = edge_weight[0, 0]
    n_live = weights.shape[0]
    order = jnp.arange(n_live, dtype=jnp.int32)
    hit = (tile_slot[0, 0][None, :] == jnp.arange(n_wide * n_rep, dtype=jnp.int32)[:, None]) & (
        order < tile_count[0, 0]
    )[None, :]
    inv = jnp.min(jnp.where(hit, order[None, :], n_live), axis=1)
    vmem = pl.BlockSpec(memory_space=pltpu.VMEM)
    dma = pltpu.SemaphoreType.DMA
    return pl.pallas_call(
        layer_kernel,
        out_shape=jax.ShapeDtypeStruct((rows, width), BF16),
        in_specs=[vmem] * 4
        + [pl.BlockSpec(memory_space=pl.ANY), pl.BlockSpec(memory_space=pltpu.SMEM)],
        out_specs=vmem,
        scratch_shapes=[
            pltpu.VMEM((n_wide, rows, width), BF16),
            pltpu.VMEM((n_rep, rows, width), BF16),
            pltpu.VMEM((n_live + 1, rows, rows), BF16),
            pltpu.VMEM((n_rep, rows, width), F32),
            pltpu.VMEM((8 * rows, 4 * rows), BF16),
            pltpu.VMEM((n_rep, rows, width), BF16),
            pltpu.VMEM((2, rows, width), BF16),
            pltpu.VMEM((2, rows, width), BF16),
            pltpu.VMEM((2, rows, width), BF16),
            pltpu.VMEM((2, rows, width), BF16),
            pltpu.VMEM((2, rows, width), BF16),
            dma((32,)), dma((32,)), dma((32,)), dma((16,)), dma((12,)), dma((4,)), dma((3,)),
            dma((8,)), dma((64,)), dma((32,)),
            dma((n_rep,)), dma((7,)), dma((7,)), dma((7,)), dma,
        ],
        compiler_params=pltpu.CompilerParams(
            collective_id=0, has_side_effects=True, vmem_limit_bytes=56 * 2**20
        ),
    )(features, w_query, w_key, w_out, weights, inv)


def solution(mesh):
    in_specs = (
        P(("wide", "rep"), None),
        P(),
        P(),
        P(),
        P("wide", "rep", None, None, None),
        P("wide", "rep", None),
        P("wide", "rep"),
    )
    out_specs = P(("wide", "rep"), None)
    return jax.shard_map(
        on_device, mesh=mesh, in_specs=in_specs, out_specs=out_specs, check_vma=False
    )
```

```python
import jax
import jax.numpy as jnp
from jax import lax
from jax.experimental import pallas as pl
from jax.experimental.pallas import tpu as pltpu
from jax.sharding import PartitionSpec as P

F32 = jnp.float32
BF16 = jnp.bfloat16
MESH = pl.DeviceIdType.MESH

NY, NZ, NX = 8, 4, 4
ROWS_A = 96


def layer_kernel(
    feat, w_query, w_key, w_out, edge, inv, out,
    src, qry, wts, total, pbuf, part, far, near, merged, joined, zbuf,
    recv_a, recv_b, recv_ca, recv_cb, ring_pa, ring_sa, ring_pb, ring_sb, line_a, line_b,
    send_ca, send_cb,
    qrecv, qsend, xrecv, xsend, local,
):
    n_wide = src.shape[0]
    rows, width = feat.shape
    n_live = edge.shape[0]
    factor = 1.0 / float(width) ** 0.5
    w, r = lax.axis_index("wide"), lax.axis_index("rep")
    c, zl, y = w % 2, (w // 2) % NZ, w // 8
    zh, x = r // NX, r % NX
    zo = 1 - zh
    sgn = 1 - 2 * c
    top = zl // 2
    inner = zl * (1 - top) + (NZ - 1 - zl) * top

    def block_of(yy, zz):
        return ((yy + 2 * NY) % NY) * 8 + zz * 2 + c

    def rep_of(zz, xx):
        return zz * NX + (xx + NX) % NX

    def line_at(p):
        return top * (NZ - 1) + (1 - 2 * top) * (p + inner * (1 - p // 2) * (1 - 2 * p))

    ahead = (block_of(y + sgn, zl), r)
    behind = (block_of(y - sgn, zl), r)
    partner = (w + sgn, r)
    above, below = (w + 2, r), (w - 2, r)
    x_ahead = (w, rep_of(zh, x + sgn))
    x_behind = (w, rep_of(zh, x - sgn))
    x_far = (w, rep_of(zh, x + 2))
    z_far = (w, rep_of(zo, x))
    has_above, has_below = zl < NZ - 1, zl > 0

    def remote(a, b, s_sem, r_sem, device):
        return pltpu.make_async_remote_copy(
            src_ref=a, dst_ref=b, send_sem=s_sem, recv_sem=r_sem,
            device_id=device, device_id_type=MESH,
        )

    def move_a(b, s_sem, device):
        ref = src.at[b, pl.ds(0, ROWS_A)]
        return remote(ref, ref, s_sem, recv_a.at[b // 2], device)

    def move_b(b, s_sem, device):
        ref = src.at[b, pl.ds(ROWS_A, rows - ROWS_A)]
        return remote(ref, ref, s_sem, recv_b.at[b // 2], device)

    def move_ca(b, k):
        ref = src.at[b, pl.ds(0, ROWS_A)]
        return remote(ref, ref, send_ca.at[k], recv_ca.at[b // 2], partner)

    def move_cb(b, k):
        ref = src.at[b, pl.ds(ROWS_A, rows - ROWS_A)]
        return remote(ref, ref, send_cb.at[k], recv_cb.at[b // 2], partner)

    def qmove(b, k, device):
        return remote(qry.at[b], qry.at[b], qsend.at[k], qrecv.at[b], device)

    barrier = pltpu.get_barrier_semaphore()

    def greet(device):
        pl.semaphore_signal(barrier, inc=1, device_id=device, device_id_type=MESH)

    talk = [ahead, behind, partner, x_ahead, x_behind, x_far, z_far]
    for device in talk:
        greet(device)

    @pl.when(has_above)
    def _():
        greet(above)

    @pl.when(has_below)
    def _():
        greet(below)

    load = pltpu.make_async_copy(edge, wts.at[pl.ds(0, n_live)], local)
    load.start()
    wts[n_live] = jnp.zeros(wts.shape[1:], BF16)
    src[w] = jnp.dot(feat[...], w_key[...], preferred_element_type=F32).astype(BF16)
    qry[r] = jnp.dot(feat[...], w_query[...], preferred_element_type=F32).astype(BF16)
    total[...] = jnp.zeros_like(total)
    pl.semaphore_wait(barrier, len(talk) + 1 + inner)

    def line_pass(move, b, zz, sems, k):
        @pl.when((zz <= zl) & has_above)
        def _():
            move(b, sems.at[2 * k], above).start()

        @pl.when((zz >= zl) & has_below)
        def _():
            move(b, sems.at[2 * k + 1], below).start()

    def got_a(b):
        move_a(b, ring_pa.at[0], ahead).wait_recv()

    def got_b(b):
        move_b(b, ring_pb.at[0], ahead).wait_recv()

    def qgot(b):
        qmove(b, 0, x_ahead).wait_recv()

    def when(cond, body):
        if isinstance(cond, bool):
            if cond:
                body()
        else:
            pl.when(cond)(body)

    def take_near(m):
        zz = line_at(m)
        b = block_of(y, zz)
        if m:
            got_a(b)
        move_a(b, ring_pa.at[m], ahead).start()
        move_a(b, ring_sa.at[m], behind).start()
        line_pass(move_a, b, zz, line_a, m)
        move_ca(b, m).start()

    def take_second(m):
        d, p = m // NZ, m % NZ
        b = block_of(y + sgn * d, line_at(p))
        got_a(b)
        when(d < 3, lambda: move_a(b, ring_sa.at[m], behind).start())
        move_ca(b, m).start()

    def take_first(n):
        d, p = 1 + n // NZ, n % NZ
        b = block_of(y - sgn * d, line_at(p))
        got_a(b)
        when(d < 4, lambda: move_a(b, ring_pa.at[NZ + n], ahead).start())
        move_ca(b, 16 + n).start()

    def rest(d, p):
        zz = line_at(p)

        def near():
            b = block_of(y, zz)
            if p:
                got_b(b)
            else:
                move_b(b, ring_pb.at[0], ahead).start()
                move_b(b, ring_sb.at[0], behind).start()
            line_pass(move_b, b, zz, line_b, p)
            move_cb(b, p).start()

        def second():
            b = block_of(y + sgn * d, zz)
            got_b(b)
            if p == 0:
                when(d < 3, lambda: move_b(b, ring_sb.at[d], behind).start())
            line_pass(move_b, b, zz, line_b, 4 * d + p)
            move_cb(b, 4 * d + p).start()

        def first():
            b = block_of(y - sgn * d, zz)
            got_b(b)
            if p == 0:
                when(d < 4, lambda: move_b(b, ring_pb.at[d], ahead).start())
            line_pass(move_b, b, zz, line_b, 12 + 4 * d + p)
            move_cb(b, 12 + 4 * d + p).start()

        when(d == 0, near)
        when((d >= 1) & (d <= 3), second)
        when((d >= 1) & (d <= 4), first)

    def diagonal(k):
        for p in range(NZ):
            rest(k - p, p)

    def event(n):
        take_second(NZ + n)
        take_first(n)

    def near_block(p):
        return block_of(y, line_at(p))

    def second_block(n):
        return block_of(y + sgn * (1 + n // NZ), line_at(n % NZ))

    def first_block(n):
        return block_of(y - sgn * (1 + n // NZ), line_at(n % NZ))

    def tiles(b1, b2, first, count, wait=True):
        if wait:
            for b in (b1, b2):
                move_ca(b + sgn, 0).wait_recv()
                move_cb(b + sgn, 0).wait_recv()
        blocks = [b1 - c, b1 - c + 1, b2 - c, b2 - c + 1]
        sources = jnp.concatenate([src[b] for b in blocks], axis=0)
        scores = lax.dot_general(
            qry[pl.ds(first, count)].reshape(count * rows, width), sources,
            (((1,), (1,)), ((), ())), preferred_element_type=F32,
        )
        for i in range(count):
            for k in range(4):
                slot = ((w - blocks[k] + n_wide) % n_wide) * 8 + first + i
                tile = wts[inv[slot]].astype(F32)
                piece = scores[i * rows:(i + 1) * rows, k * rows:(k + 1) * rows]
                pbuf[i * rows:(i + 1) * rows, k * rows:(k + 1) * rows] = (
                    jnp.tanh(piece * factor) * tile
                ).astype(BF16)
        total[pl.ds(first, count)] += jnp.dot(
            pbuf[:count * rows], sources, preferred_element_type=F32
        ).reshape(count, rows, width)

    def ring_tiles(n):
        tiles(second_block(n), first_block(n), 0, 8)

    def loop(lo, hi, body):
        def step(i, carry):
            body(i)
            return carry

        lax.fori_loop(lo, hi, step, 0)

    take_near(0)
    qmove(r, 0, z_far).start()
    qmove(r, 1, x_ahead).start()
    qmove(r, 2, x_behind).start()
    qmove(r, 3, x_far).start()
    rest(0, 0)
    take_near(1)
    event(0)
    diagonal(1)
    take_near(2)
    event(1)
    take_near(3)
    event(2)
    diagonal(2)
    qz = rep_of(zo, x)
    qgot(qz)
    qmove(qz, 4, x_ahead).start()
    qmove(qz, 5, x_behind).start()
    qmove(qz, 6, x_far).start()
    event(3)
    event(4)
    diagonal(3)
    event(5)
    for zz in (zh, zo):
        for k in (sgn, -sgn, 2):
            qgot(rep_of(zz, x + k))
    load.wait()
    loop(0, 2, lambda k: tiles(near_block(2 * k), near_block(2 * k + 1), 0, 8))

    def both(t):
        event(6 + 2 * t)
        diagonal(4 + t)
        loop(4 * t, 4 * t + 2, ring_tiles)
        event(7 + 2 * t)
        loop(4 * t + 2, 4 * t + 4, ring_tiles)

    loop(0, 3, both)
    diagonal(7)
    take_first(12)
    take_first(13)
    tiles(first_block(12), first_block(13), 0, 8)
    take_first(14)
    take_first(15)

    def xcopy(a, b, k, device):
        return remote(a, b, xsend.at[k], xrecv.at[k], device)

    zs = (zo, zh)
    c_far = [xcopy(part.at[rep_of(zs[k], x + 2)], far.at[k], k, x_ahead) for k in (0, 1)]
    c_near = [xcopy(part.at[rep_of(zs[k], x - sgn)], near.at[k], 2 + k, x_behind) for k in (0, 1)]
    c_join = [xcopy(merged.at[k], joined.at[k], 4 + k, x_ahead) for k in (0, 1)]
    c_z = xcopy(zbuf.at[0], zbuf.at[1], 6, z_far)

    for k in (0, 1):
        tiles(first_block(14), first_block(15), 4 * zs[k], 4, k == 0)
        for place in (rep_of(zs[k], x + 2), rep_of(zs[k], x - sgn)):
            part[place] = total[place].astype(BF16)
        c_far[k].start()
        c_near[k].start()
    for k in (0, 1):
        c_far[k].wait_recv()
        merged[k] = (total[rep_of(zs[k], x + sgn)] + far[k].astype(F32)).astype(BF16)
        c_join[k].start()

    def mine(k):
        c_near[k].wait_recv()
        c_join[k].wait_recv()
        return total[rep_of(zs[k], x)] + near[k].astype(F32) + joined[k].astype(F32)

    zbuf[0] = mine(0).astype(BF16)
    c_z.start()
    own = mine(1)
    c_z.wait_recv()
    message = (own + zbuf[1].astype(F32)).astype(BF16)
    out[...] = (
        feat[...].astype(F32) + jnp.dot(message, w_out[...], preferred_element_type=F32)
    ).astype(BF16)

    for copy in c_far + c_near + c_join + [c_z]:
        copy.wait_send()
    loop(0, 16, lambda k: move_a(w, ring_pa.at[k], ahead).wait_send())
    loop(0, 12, lambda k: move_a(w, ring_sa.at[k], behind).wait_send())
    loop(0, 4, lambda k: move_b(w, ring_pb.at[k], ahead).wait_send())
    loop(0, 3, lambda k: move_b(w, ring_sb.at[k], behind).wait_send())
    loop(0, 32, lambda k: move_ca(w, k).wait_send())
    loop(0, 32, lambda k: move_cb(w, k).wait_send())
    loop(0, 7, lambda k: qmove(r, k, x_ahead).wait_send())

    def line_sent(move, sems, k):
        zz = line_at(k % NZ)

        @pl.when((zz <= zl) & has_above)
        def _():
            move(w, sems.at[2 * k], above).wait_send()

        @pl.when((zz >= zl) & has_below)
        def _():
            move(w, sems.at[2 * k + 1], below).wait_send()

    loop(0, 4, lambda k: line_sent(move_a, line_a, k))
    loop(0, 32, lambda k: line_sent(move_b, line_b, k))


def on_device(features, w_query, w_key, w_out, edge_weight, tile_slot, tile_count):
    rows, width = features.shape
    n_wide = lax.axis_size("wide")
    n_rep = lax.axis_size("rep")
    weights = edge_weight[0, 0]
    n_live = weights.shape[0]
    order = jnp.arange(n_live, dtype=jnp.int32)
    hit = (tile_slot[0, 0][None, :] == jnp.arange(n_wide * n_rep, dtype=jnp.int32)[:, None]) & (
        order < tile_count[0, 0]
    )[None, :]
    inv = jnp.min(jnp.where(hit, order[None, :], n_live), axis=1)
    vmem = pl.BlockSpec(memory_space=pltpu.VMEM)
    dma = pltpu.SemaphoreType.DMA
    return pl.pallas_call(
        layer_kernel,
        out_shape=jax.ShapeDtypeStruct((rows, width), BF16),
        in_specs=[vmem] * 4
        + [pl.BlockSpec(memory_space=pl.ANY), pl.BlockSpec(memory_space=pltpu.SMEM)],
        out_specs=vmem,
        scratch_shapes=[
            pltpu.VMEM((n_wide, rows, width), BF16),
            pltpu.VMEM((n_rep, rows, width), BF16),
            pltpu.VMEM((n_live + 1, rows, rows), BF16),
            pltpu.VMEM((n_rep, rows, width), F32),
            pltpu.VMEM((8 * rows, 4 * rows), BF16),
            pltpu.VMEM((n_rep, rows, width), BF16),
            pltpu.VMEM((2, rows, width), BF16),
            pltpu.VMEM((2, rows, width), BF16),
            pltpu.VMEM((2, rows, width), BF16),
            pltpu.VMEM((2, rows, width), BF16),
            pltpu.VMEM((2, rows, width), BF16),
            dma((32,)), dma((32,)), dma((32,)), dma((32,)), dma((16,)), dma((12,)), dma((4,)),
            dma((3,)), dma((8,)), dma((64,)), dma((32,)), dma((32,)),
            dma((n_rep,)), dma((7,)), dma((7,)), dma((7,)), dma,
        ],
        compiler_params=pltpu.CompilerParams(
            collective_id=0, has_side_effects=True, vmem_limit_bytes=56 * 2**20
        ),
    )(features, w_query, w_key, w_out, weights, inv)


def solution(mesh):
    in_specs = (
        P(("wide", "rep"), None),
        P(),
        P(),
        P(),
        P("wide", "rep", None, None, None),
        P("wide", "rep", None),
        P("wide", "rep"),
    )
    out_specs = P(("wide", "rep"), None)
    return jax.shard_map(
        on_device, mesh=mesh, in_specs=in_specs, out_specs=out_specs, check_vma=False
    )
```

```python
import jax
import jax.numpy as jnp
from jax import lax
from jax.experimental import pallas as pl
from jax.experimental.pallas import tpu as pltpu
from jax.sharding import PartitionSpec as P

F32 = jnp.float32
BF16 = jnp.bfloat16
MESH = pl.DeviceIdType.MESH

NY, NZ, NX = 8, 4, 4
ROWS_A = 96


def layer_kernel(
    feat, w_query, w_key, w_out, edge, slots, count, out,
    src, qry, wts, total, pbuf, part, far, near, merged, joined, zbuf,
    recv_a, recv_b, recv_ca, recv_cb, ring_pa, ring_sa, ring_pb, ring_sb, line_a, line_b,
    send_ca, send_cb,
    qrecv, qsend, xrecv, xsend, local, found, table, listed,
):
    n_wide = src.shape[0]
    rows, width = feat.shape
    n_live = edge.shape[0]
    factor = 1.0 / float(width) ** 0.5
    w, r = lax.axis_index("wide"), lax.axis_index("rep")
    c, zl, y = w % 2, (w // 2) % NZ, w // 8
    zh, x = r // NX, r % NX
    zo = 1 - zh
    sgn = 1 - 2 * c
    top = zl // 2
    inner = zl * (1 - top) + (NZ - 1 - zl) * top

    def block_of(yy, zz):
        return ((yy + 2 * NY) % NY) * 8 + zz * 2 + c

    def rep_of(zz, xx):
        return zz * NX + (xx + NX) % NX

    def line_at(p):
        return top * (NZ - 1) + (1 - 2 * top) * (p + inner * (1 - p // 2) * (1 - 2 * p))

    ahead = (block_of(y + sgn, zl), r)
    behind = (block_of(y - sgn, zl), r)
    partner = (w + sgn, r)
    above, below = (w + 2, r), (w - 2, r)
    x_ahead = (w, rep_of(zh, x + sgn))
    x_behind = (w, rep_of(zh, x - sgn))
    x_far = (w, rep_of(zh, x + 2))
    z_far = (w, rep_of(zo, x))
    has_above, has_below = zl < NZ - 1, zl > 0

    def remote(a, b, s_sem, r_sem, device):
        return pltpu.make_async_remote_copy(
            src_ref=a, dst_ref=b, send_sem=s_sem, recv_sem=r_sem,
            device_id=device, device_id_type=MESH,
        )

    def move_a(b, s_sem, device):
        ref = src.at[b, pl.ds(0, ROWS_A)]
        return remote(ref, ref, s_sem, recv_a.at[b // 2], device)

    def move_b(b, s_sem, device):
        ref = src.at[b, pl.ds(ROWS_A, rows - ROWS_A)]
        return remote(ref, ref, s_sem, recv_b.at[b // 2], device)

    def move_ca(b, k):
        ref = src.at[b, pl.ds(0, ROWS_A)]
        return remote(ref, ref, send_ca.at[k], recv_ca.at[b // 2], partner)

    def move_cb(b, k):
        ref = src.at[b, pl.ds(ROWS_A, rows - ROWS_A)]
        return remote(ref, ref, send_cb.at[k], recv_cb.at[b // 2], partner)

    def qmove(b, k, device):
        return remote(qry.at[b], qry.at[b], qsend.at[k], qrecv.at[b], device)

    barrier = pltpu.get_barrier_semaphore()

    def greet(device):
        pl.semaphore_signal(barrier, inc=1, device_id=device, device_id_type=MESH)

    talk = [ahead, behind, partner, x_ahead, x_behind, x_far, z_far]
    for device in talk:
        greet(device)

    @pl.when(has_above)
    def _():
        greet(above)

    @pl.when(has_below)
    def _():
        greet(below)

    load = pltpu.make_async_copy(edge, wts.at[pl.ds(0, n_live)], local)
    load.start()
    wts[n_live] = jnp.zeros(wts.shape[1:], BF16)
    src[w] = jnp.dot(feat[...], w_key[...], preferred_element_type=F32).astype(BF16)
    qry[r] = jnp.dot(feat[...], w_query[...], preferred_element_type=F32).astype(BF16)
    total[...] = jnp.zeros_like(total)

    numbers = lax.broadcasted_iota(jnp.int32, found.shape, 0) * found.shape[1]
    numbers += lax.broadcasted_iota(jnp.int32, found.shape, 1)
    live = count[0]

    def look(t, held):
        return jnp.where(numbers == jnp.where(t < live, slots[t], -1), t, held)

    found[...] = lax.fori_loop(0, n_live, look, jnp.full(found.shape, n_live, jnp.int32))
    pl.semaphore_wait(barrier, len(talk) + 1 + inner)

    fetch = pltpu.make_async_copy(found, table, listed)

    def line_pass(move, b, zz, sems, k):
        @pl.when((zz <= zl) & has_above)
        def _():
            move(b, sems.at[2 * k], above).start()

        @pl.when((zz >= zl) & has_below)
        def _():
            move(b, sems.at[2 * k + 1], below).start()

    def got_a(b):
        move_a(b, ring_pa.at[0], ahead).wait_recv()

    def got_b(b):
        move_b(b, ring_pb.at[0], ahead).wait_recv()

    def qgot(b):
        qmove(b, 0, x_ahead).wait_recv()

    def when(cond, body):
        if isinstance(cond, bool):
            if cond:
                body()
        else:
            pl.when(cond)(body)

    def take_near(m):
        zz = line_at(m)
        b = block_of(y, zz)
        if m:
            got_a(b)
        move_a(b, ring_pa.at[m], ahead).start()
        move_a(b, ring_sa.at[m], behind).start()
        line_pass(move_a, b, zz, line_a, m)
        move_ca(b, m).start()

    def take_second(m):
        d, p = m // NZ, m % NZ
        b = block_of(y + sgn * d, line_at(p))
        got_a(b)
        when(d < 3, lambda: move_a(b, ring_sa.at[m], behind).start())
        move_ca(b, m).start()

    def take_first(n):
        d, p = 1 + n // NZ, n % NZ
        b = block_of(y - sgn * d, line_at(p))
        got_a(b)
        when(d < 4, lambda: move_a(b, ring_pa.at[NZ + n], ahead).start())
        move_ca(b, 16 + n).start()

    def rest(d, p):
        zz = line_at(p)

        def near():
            b = block_of(y, zz)
            if p:
                got_b(b)
            else:
                move_b(b, ring_pb.at[0], ahead).start()
                move_b(b, ring_sb.at[0], behind).start()
            line_pass(move_b, b, zz, line_b, p)
            move_cb(b, p).start()

        def second():
            b = block_of(y + sgn * d, zz)
            got_b(b)
            if p == 0:
                when(d < 3, lambda: move_b(b, ring_sb.at[d], behind).start())
            line_pass(move_b, b, zz, line_b, 4 * d + p)
            move_cb(b, 4 * d + p).start()

        def first():
            b = block_of(y - sgn * d, zz)
            got_b(b)
            if p == 0:
                when(d < 4, lambda: move_b(b, ring_pb.at[d], ahead).start())
            line_pass(move_b, b, zz, line_b, 12 + 4 * d + p)
            move_cb(b, 12 + 4 * d + p).start()

        when(d == 0, near)
        when((d >= 1) & (d <= 3), second)
        when((d >= 1) & (d <= 4), first)

    def diagonal(k):
        for p in range(NZ):
            rest(k - p, p)

    def event(n):
        take_second(NZ + n)
        take_first(n)

    def near_block(p):
        return block_of(y, line_at(p))

    def second_block(n):
        return block_of(y + sgn * (1 + n // NZ), line_at(n % NZ))

    def first_block(n):
        return block_of(y - sgn * (1 + n // NZ), line_at(n % NZ))

    def tiles(b1, b2, first, count, wait=True):
        if wait:
            for b in (b1, b2):
                move_ca(b + sgn, 0).wait_recv()
                move_cb(b + sgn, 0).wait_recv()
        blocks = [b1 - c, b1 - c + 1, b2 - c, b2 - c + 1]
        sources = jnp.concatenate([src[b] for b in blocks], axis=0)
        scores = lax.dot_general(
            qry[pl.ds(first, count)].reshape(count * rows, width), sources,
            (((1,), (1,)), ((), ())), preferred_element_type=F32,
        )
        for i in range(count):
            for k in range(4):
                slot = ((w - blocks[k] + n_wide) % n_wide) * 8 + first + i
                tile = wts[table[slot // 128, slot % 128]].astype(F32)
                piece = scores[i * rows:(i + 1) * rows, k * rows:(k + 1) * rows]
                pbuf[i * rows:(i + 1) * rows, k * rows:(k + 1) * rows] = (
                    jnp.tanh(piece * factor) * tile
                ).astype(BF16)
        total[pl.ds(first, count)] += jnp.dot(
            pbuf[:count * rows], sources, preferred_element_type=F32
        ).reshape(count, rows, width)

    def ring_tiles(n):
        tiles(second_block(n), first_block(n), 0, 8)

    def loop(lo, hi, body):
        def step(i, carry):
            body(i)
            return carry

        lax.fori_loop(lo, hi, step, 0)

    take_near(0)
    qmove(r, 0, z_far).start()
    qmove(r, 1, x_ahead).start()
    qmove(r, 2, x_behind).start()
    qmove(r, 3, x_far).start()
    rest(0, 0)
    fetch.start()
    take_near(1)
    event(0)
    diagonal(1)
    take_near(2)
    event(1)
    take_near(3)
    event(2)
    diagonal(2)
    qz = rep_of(zo, x)
    qgot(qz)
    qmove(qz, 4, x_ahead).start()
    qmove(qz, 5, x_behind).start()
    qmove(qz, 6, x_far).start()
    event(3)
    event(4)
    diagonal(3)
    event(5)
    for zz in (zh, zo):
        for k in (sgn, -sgn, 2):
            qgot(rep_of(zz, x + k))
    load.wait()
    fetch.wait()
    loop(0, 2, lambda k: tiles(near_block(2 * k), near_block(2 * k + 1), 0, 8))

    def both(t):
        event(6 + 2 * t)
        diagonal(4 + t)
        loop(4 * t, 4 * t + 2, ring_tiles)
        event(7 + 2 * t)
        loop(4 * t + 2, 4 * t + 4, ring_tiles)

    loop(0, 3, both)
    diagonal(7)
    take_first(12)
    take_first(13)
    tiles(first_block(12), first_block(13), 0, 8)
    take_first(14)
    take_first(15)

    def xcopy(a, b, k, device):
        return remote(a, b, xsend.at[k], xrecv.at[k], device)

    zs = (zo, zh)
    c_far = [xcopy(part.at[rep_of(zs[k], x + 2)], far.at[k], k, x_ahead) for k in (0, 1)]
    c_near = [xcopy(part.at[rep_of(zs[k], x - sgn)], near.at[k], 2 + k, x_behind) for k in (0, 1)]
    c_join = [xcopy(merged.at[k], joined.at[k], 4 + k, x_ahead) for k in (0, 1)]
    c_z = xcopy(zbuf.at[0], zbuf.at[1], 6, z_far)

    for k in (0, 1):
        tiles(first_block(14), first_block(15), 4 * zs[k], 4, k == 0)
        for place in (rep_of(zs[k], x + 2), rep_of(zs[k], x - sgn)):
            part[place] = total[place].astype(BF16)
        c_near[k].start()
        if k == 0:
            c_far[0].start()

    def join(k):
        c_far[k].wait_recv()
        merged[k] = (total[rep_of(zs[k], x + sgn)] + far[k].astype(F32)).astype(BF16)
        c_join[k].start()

    join(0)
    c_far[1].start()

    def mine(k):
        c_near[k].wait_recv()
        c_join[k].wait_recv()
        return total[rep_of(zs[k], x)] + near[k].astype(F32) + joined[k].astype(F32)

    zbuf[0] = mine(0).astype(BF16)
    c_z.start()
    join(1)
    own = mine(1)
    c_z.wait_recv()
    message = (own + zbuf[1].astype(F32)).astype(BF16)
    out[...] = (
        feat[...].astype(F32) + jnp.dot(message, w_out[...], preferred_element_type=F32)
    ).astype(BF16)

    for copy in c_far + c_near + c_join + [c_z]:
        copy.wait_send()
    loop(0, 16, lambda k: move_a(w, ring_pa.at[k], ahead).wait_send())
    loop(0, 12, lambda k: move_a(w, ring_sa.at[k], behind).wait_send())
    loop(0, 4, lambda k: move_b(w, ring_pb.at[k], ahead).wait_send())
    loop(0, 3, lambda k: move_b(w, ring_sb.at[k], behind).wait_send())
    loop(0, 32, lambda k: move_ca(w, k).wait_send())
    loop(0, 32, lambda k: move_cb(w, k).wait_send())
    loop(0, 7, lambda k: qmove(r, k, x_ahead).wait_send())

    def line_sent(move, sems, k):
        zz = line_at(k % NZ)

        @pl.when((zz <= zl) & has_above)
        def _():
            move(w, sems.at[2 * k], above).wait_send()

        @pl.when((zz >= zl) & has_below)
        def _():
            move(w, sems.at[2 * k + 1], below).wait_send()

    loop(0, 4, lambda k: line_sent(move_a, line_a, k))
    loop(0, 32, lambda k: line_sent(move_b, line_b, k))


def on_device(features, w_query, w_key, w_out, edge_weight, tile_slot, tile_count):
    rows, width = features.shape
    n_wide = lax.axis_size("wide")
    n_rep = lax.axis_size("rep")
    weights = edge_weight[0, 0]
    n_live = weights.shape[0]
    vmem = pl.BlockSpec(memory_space=pltpu.VMEM)
    dma = pltpu.SemaphoreType.DMA
    return pl.pallas_call(
        layer_kernel,
        out_shape=jax.ShapeDtypeStruct((rows, width), BF16),
        in_specs=[vmem] * 4
        + [pl.BlockSpec(memory_space=pl.ANY)]
        + [pl.BlockSpec(memory_space=pltpu.SMEM)] * 2,
        out_specs=vmem,
        scratch_shapes=[
            pltpu.VMEM((n_wide, rows, width), BF16),
            pltpu.VMEM((n_rep, rows, width), BF16),
            pltpu.VMEM((n_live + 1, rows, rows), BF16),
            pltpu.VMEM((n_rep, rows, width), F32),
            pltpu.VMEM((8 * rows, 4 * rows), BF16),
            pltpu.VMEM((n_rep, rows, width), BF16),
            pltpu.VMEM((2, rows, width), BF16),
            pltpu.VMEM((2, rows, width), BF16),
            pltpu.VMEM((2, rows, width), BF16),
            pltpu.VMEM((2, rows, width), BF16),
            pltpu.VMEM((2, rows, width), BF16),
            dma((32,)), dma((32,)), dma((32,)), dma((32,)), dma((16,)), dma((12,)), dma((4,)),
            dma((3,)), dma((8,)), dma((64,)), dma((32,)), dma((32,)),
            dma((n_rep,)), dma((7,)), dma((7,)), dma((7,)), dma,
            pltpu.VMEM((n_wide * n_rep // 128, 128), jnp.int32),
            pltpu.SMEM((n_wide * n_rep // 128, 128), jnp.int32), dma,
        ],
        compiler_params=pltpu.CompilerParams(
            collective_id=0, has_side_effects=True, vmem_limit_bytes=56 * 2**20
        ),
    )(features, w_query, w_key, w_out, weights, tile_slot[0, 0], tile_count[0])


def solution(mesh):
    in_specs = (
        P(("wide", "rep"), None),
        P(),
        P(),
        P(),
        P("wide", "rep", None, None, None),
        P("wide", "rep", None),
        P("wide", "rep"),
    )
    out_specs = P(("wide", "rep"), None)
    return jax.shard_map(
        on_device, mesh=mesh, in_specs=in_specs, out_specs=out_specs, check_vma=False
    )
```
